256 devices in a mesh: strat: 32 (over z, y_hi, core), grp: 8 (over x, y_lo).
Axes of the slice: x: 4, y: 4 (y_hi: 2, y_lo: 2; y = y_hi * 2 + y_lo), z: 8, core: 2. Of those that a mesh axis runs over, the one named last changes fastest.
Arguments:
- user_factors: float32 [262144, 256], P(('strat', 'grp')), may hold values from -1.5 to 1.5
- item_factors: float32 [131072, 256], P('strat'), may hold values from -1.5 to 1.5
- tile_coords: int32 [32, 8, 3, 2, 16], P('strat', 'grp'), may hold values from 0 to 31, as said below
- tile_counts: int32 [32, 8, 3], P('strat', 'grp'), may hold values from 5 to 16, as said below
- tile_values: bfloat16 [32, 8, 3, 16, 128, 128], P('strat', 'grp'), may hold values from 0 to 10
Outputs:
- users_out: float32 [262144, 256], P(('strat', 'grp'))
- items_out: float32 [131072, 256], P('strat')
The draws below stay inside these ranges and needn't reach their ends.
Inputs may be any that keep to these rules, and one draw needn't show every extreme that they name: `tile_coords`: each list names distinct tiles; user tiles lie below 8 and item tiles below 32; entries at and after the count are ignored. `tile_counts`: in every sub-epoch some device has exactly 16 live tiles.
All inputs are finite; a program needn't handle non-finite values.
Results may differ from the reference program's by a relative error of at most 0.0018.
Values sent between devices are 32-bit elements; how exact they have to be, the bound alone decides.
A program may use at most 64 MiB of HBM per device.

```python
import jax
import jax.numpy as jnp
from jax import lax

RANK = 256
TILE = 128
USERS_DEV = 1024
SLAB_ITEMS = 4096
TILES_MAX = 16
SUBEPOCHS = 3
STRATA = 32
MEMBERS = 8


def draw_tile_coords(key, part):
    user_tiles = USERS_DEV // TILE
    item_tiles = SLAB_ITEMS // TILE
    keys = jax.random.split(jax.random.fold_in(key, 11), STRATA * MEMBERS * SUBEPOCHS)
    picks = jax.vmap(lambda k: jax.random.permutation(k, user_tiles * item_tiles)[:TILES_MAX])(keys)
    picks = picks.astype(jnp.int32)
    pairs = jnp.stack([picks // item_tiles, picks % item_tiles], axis=1)
    return pairs.reshape(STRATA, MEMBERS, SUBEPOCHS, 2, TILES_MAX).astype(jnp.int32)


def draw_tile_counts(key, part):
    low = max(1, TILES_MAX // 3)
    base = jax.random.randint(jax.random.fold_in(key, 21), (STRATA * MEMBERS, SUBEPOCHS), low, TILES_MAX + 1).astype(jnp.int32)
    busiest = jax.random.randint(jax.random.fold_in(key, 22), (SUBEPOCHS,), 0, STRATA * MEMBERS).astype(jnp.int32)
    base = base.at[busiest, jnp.arange(SUBEPOCHS)].set(TILES_MAX)
    return base.reshape(STRATA, MEMBERS, SUBEPOCHS).astype(jnp.int32)


def draw_tile_values(key, part):
    shape = (STRATA, MEMBERS, SUBEPOCHS, TILES_MAX, TILE, TILE)
    seen = jax.random.uniform(jax.random.fold_in(key, 31), shape, jnp.float32)
    level = jax.random.uniform(jax.random.fold_in(key, 32), shape, jnp.float32)
    values = jnp.where(seen < 0.4, jnp.exp(level * jnp.log(4.0)), 0.0)
    return values.astype(jnp.bfloat16)


def block_scale(stream_key, extent, pieces, smallest, top_value):
    def one(dim, parts):
        draws = jax.random.uniform(jax.random.fold_in(jax.random.fold_in(stream_key, 6), dim), (parts,), jnp.float32, smallest / len(pieces), top_value / len(pieces))
        return jnp.repeat(jnp.exp(draws), extent[dim] // parts).reshape((-1,) + (1,) * (len(extent) - dim - 1))

    factor_of = one(*pieces[0])
    for cut in pieces[1:]:
        factor_of = factor_of * one(*cut)
    return factor_of


def scatter_about(key, extent, spread, bound, shards=(), kind=jnp.bfloat16):
    gain = block_scale(key, extent, shards, -0.22, 0.18) if shards else 1.0
    drawn = jax.random.normal(key, extent, jnp.float32) * spread * gain
    return jnp.minimum(jnp.maximum(drawn, -bound), bound).astype(kind)


def setup_inputs(seed: int = 0) -> dict:
    seeds = jax.random.split(jax.random.key(seed), 6)
    return {
        "user_factors": scatter_about(seeds[0], (STRATA * MEMBERS * USERS_DEV, RANK), 0.25, 1.5, ((0, 256),), jnp.float32),
        "item_factors": scatter_about(seeds[1], (STRATA * SLAB_ITEMS, RANK), 0.25, 1.5, ((0, 32),), jnp.float32),
        "tile_coords": draw_tile_coords(jax.random.fold_in(seeds[5], 71), 0),
        "tile_counts": draw_tile_counts(jax.random.fold_in(seeds[5], 71), 0),
        "tile_values": draw_tile_values(jax.random.fold_in(seeds[5], 71), 0),
    }


def tile_terms(users_blk, slab, coords, count, values):
    high = lax.Precision.HIGHEST
    user_b = users_blk.astype(jnp.bfloat16).astype(jnp.float32)
    slab_b = slab.astype(jnp.bfloat16).astype(jnp.float32)
    user_tiles = user_b.shape[0] // TILE
    item_tiles = slab_b.shape[0] // TILE
    urows = jnp.take(user_b.reshape(user_tiles, TILE, RANK), coords[0], axis=0)
    irows = jnp.take(slab_b.reshape(item_tiles, TILE, RANK), coords[1], axis=0)
    predicted = jnp.einsum("nrk,nck->nrc", urows, irows, precision=high)
    resid = lax.optimization_barrier((values.astype(jnp.float32) - predicted).astype(jnp.bfloat16))
    resid = resid.astype(jnp.float32)
    user_part = jnp.einsum("nrc,nck->nrk", resid, irows, precision=high)
    item_part = jnp.einsum("nrc,nrk->nck", resid, urows, precision=high)
    live = jnp.arange(coords.shape[1]) < count
    one_user = ((coords[0][:, None] == jnp.arange(user_tiles)[None, :]) & live[:, None]).astype(jnp.float32)
    one_item = ((coords[1][:, None] == jnp.arange(item_tiles)[None, :]) & live[:, None]).astype(jnp.float32)
    user_grad = jnp.einsum("nt,nrk->trk", one_user, user_part, precision=high).reshape(-1, RANK)
    item_grad = jnp.einsum("nt,nrk->trk", one_item, item_part, precision=high).reshape(-1, RANK)
    return user_grad, item_grad


def reference(user_factors, item_factors, tile_coords, tile_counts, tile_values):
    users = user_factors.reshape(STRATA, MEMBERS, USERS_DEV, RANK)
    held = item_factors.reshape(STRATA, SLAB_ITEMS, RANK)
    for sub in range(SUBEPOCHS):
        def one_stratum(pack):
            block, slab, coords, counts, values = pack
            grads_u, grads_i = jax.vmap(lambda u, c, n, v: tile_terms(u, slab, c, n, v))(block, coords, counts, values)
            return grads_u, jnp.sum(grads_i, axis=0)
        user_grad, item_grad = lax.map(one_stratum, (users, held, tile_coords[:, :, sub], tile_counts[:, :, sub], tile_values[:, :, sub]))
        users = users - 0.003 * (0.05 * users - user_grad)
        held = held - 0.003 * (0.05 * held - item_grad)
        if sub + 1 < SUBEPOCHS:
            held = jnp.roll(held, -1, axis=0)
    return users.reshape(-1, RANK), held.reshape(-1, RANK)
```

```python
import jax
import jax.numpy as jnp
from jax import lax
from jax.experimental import pallas as pl
from jax.experimental.pallas import tpu as pltpu
from jax.sharding import PartitionSpec as P

MESH = pl.DeviceIdType.MESH
F32 = jnp.float32
BF16 = jnp.bfloat16
RATE = 0.003
DECAY = 0.05
SEMS = 256


def step_of(value, grad):
    return value - RATE * (DECAY * value - grad)


def kernel(
    strata, tab_s, tab_v, users, slab, vals, users_out, items_out,
    uf, uc, uo, ug, ub, vb, res, res_t, lhs, grad, vals_out, vals_in, tab_in, tab_c,
    rb0, rb1, rb2, sib1, sib2, part, vu0, vu1, vu2, vn1, vn2, out, ssem, rsem, lsem,
):
    s, g = lax.axis_index("strat"), lax.axis_index("grp")
    core, yhi, x, ylo = s % 2, (s // 2) % 2, g // 2, g % 2
    base = s - core
    side = (ylo + yhi) % 2
    keeps = core == side
    moves = core != side
    rx, lx, ox = (x + 1) % 4, (x + 3) % 4, (x + 2) % 4
    right, left = (s, rx * 2 + ylo), (s, lx * 2 + ylo)
    sibling = (base + 1 - core, g)
    across = (s, x * 2 + 1 - ylo)
    swap = (base + 1 - core, x * 2 + 1 - ylo)
    ahead = (s + strata - 2) % strata
    behind = (s + 2) % strata

    barrier = pltpu.get_barrier_semaphore()

    def greet(device):
        pl.semaphore_signal(barrier, inc=1, device_id=device, device_id_type=MESH)

    for device in (right, left, sibling, across, swap):
        greet(device)

    @pl.when(side == 0)
    def _():
        greet((ahead, g))

    @pl.when(side == 1)
    def _():
        greet((behind, g))
        greet(((base + 2) % strata, x * 2 + 1 - ylo))

    @pl.when((side == 1) & (core == 0))
    def _():
        greet((ahead, x * 2 + 1 - ylo))
        greet((ahead + 1, x * 2 + 1 - ylo))

    pl.semaphore_wait(barrier, 6 + side * (1 + 2 * (1 - core)))

    def rc(src, dst, si, ri, device):
        return pltpu.make_async_remote_copy(
            src_ref=src, dst_ref=dst, send_sem=ssem.at[si], recv_sem=rsem.at[ri],
            device_id=device, device_id_type=MESH,
        )

    def arrived(ref, ri):
        rc(ref, ref, 0, ri, right).wait_recv()

    counts = {"s": 0, "r": 0}

    def take(kind, n):
        counts[kind] += n
        assert counts[kind] <= SEMS
        return counts[kind] - n

    def each(n, body):
        @pl.loop(0, n)
        def _(i):
            body(i)

    def residuals(tab, values):
        def one(n):
            u = ub[tab(0, 32 + n)]
            v = vb[tab(0, 48 + n)]
            guess = lax.dot_general(u, v, (((1,), (1,)), ((), ())), preferred_element_type=F32)
            left_over = values(n).astype(F32) - guess
            res[n] = left_over.astype(BF16)
            res_t[n] = left_over.T.astype(BF16)

        each(16, one)

    def item_quad(tab, q):
        for i in range(4):
            for a in range(8):
                lhs[i * 128:(i + 1) * 128, a * 128:(a + 1) * 128] = res_t[tab(a, q * 4 + i)]
        total = jnp.dot(lhs[...], ub[...].reshape(1024, 256), preferred_element_type=F32)
        grad[pl.ds(q * 4, 4)] = total.reshape(4, 128, 256)

    def user_grads(tab):
        def one(w):
            half, c = w // 4, w % 4
            for i in range(4):
                for j in range(8):
                    lhs[i * 128:(i + 1) * 128, j * 128:(j + 1) * 128] = res[tab(half * 4 + i, c * 8 + j)]
            block = vb[pl.ds(c * 8, 8)].reshape(1024, 256)
            total = jnp.dot(lhs[...], block, preferred_element_type=F32)
            spot = pl.ds(half * 4, 4)
            ug[spot] = ug[spot] + total.reshape(4, 128, 256)

        ug[...] = jnp.zeros_like(ug)
        each(8, one)

    class Ring:
        def __init__(self, tile, m, rb):
            self.tile, self.m, self.rb = tile, m, rb
            self.so, self.ro = take("s", 6 * m), take("r", 6 * m)

        def go(self, chunk, j, slot, k, device):
            return rc(grad.at[self.tile(chunk, j)], self.rb.at[slot], self.so + k, self.ro + slot, device)

        def opp_r(self, j):
            return self.go(ox, j, j, j, right)

        def opp_l(self, j):
            return self.go(ox, self.m + j, self.m + j, self.m + j, left)

        def mid_r(self, j):
            return self.go(rx, self.m + j, 3 * self.m + j, 2 * self.m + j, right)

        def mid_l(self, j):
            return self.go(lx, j, 4 * self.m + j, 3 * self.m + j, left)

        def end_r(self, j):
            return self.go(rx, j, 2 * self.m + j, 4 * self.m + j, right)

        def end_l(self, j):
            return self.go(lx, self.m + j, 5 * self.m + j, 5 * self.m + j, left)

        def landed(self, slot):
            arrived(self.rb.at[slot], self.ro + slot)

        def start_opp(self):
            each(self.m, lambda j: (self.opp_r(j).start(), self.opp_l(j).start()))

        def start_mid_r(self):
            each(self.m, lambda j: self.mid_r(j).start())

        def start_mid_l(self):
            each(self.m, lambda j: self.mid_l(j).start())

        def relay(self):
            def one(j):
                self.landed(j)
                spot = self.tile(rx, j)
                grad[spot] = grad[spot] + self.rb[j]
                self.end_r(j).start()
                self.landed(self.m + j)
                spot = self.tile(lx, self.m + j)
                grad[spot] = grad[spot] + self.rb[self.m + j]
                self.end_l(j).start()

            each(self.m, one)

        def finish(self, done):
            m = self.m

            def one(j):
                self.landed(4 * m + j)
                self.landed(2 * m + j)
                done(j, grad[self.tile(x, j)] + self.rb[2 * m + j] + self.rb[4 * m + j])
                self.landed(3 * m + j)
                self.landed(5 * m + j)
                done(m + j, grad[self.tile(x, m + j)] + self.rb[3 * m + j] + self.rb[5 * m + j])

            each(m, one)

        def drain(self):
            def one(j):
                for f in (self.opp_r, self.opp_l, self.mid_r, self.mid_l, self.end_r, self.end_l):
                    f(j).wait_send()

            each(self.m, one)

    class Spread:
        def __init__(self, buf, half, extra):
            self.buf, self.half, self.extra = buf, half, extra
            self.so, self.ro = take("s", 12), take("r", 12)

        def at(self, chunk, p):
            return self.buf.at[chunk * 8 + self.half * 4 + p]

        def own_r(self, p):
            return rc(self.at(x, p), self.at(x, p), self.so + p, self.ro + p, right)

        def own_l(self, p):
            return rc(self.at(x, p), self.at(x, p), self.so + 4 + p, self.ro + 4 + p, left)

        def fwd_r(self, p):
            return rc(self.at(lx, p), self.at(lx, p), self.so + 8 + p, self.ro + 8 + p, right)

        def fwd_l(self, p):
            return rc(self.at(rx, 2 + p), self.at(rx, 2 + p), self.so + 10 + p, self.ro + 10 + p, left)

        def own(self, p):
            self.own_r(p).start()
            self.own_l(p).start()

        def rest(self):
            def first(p):
                arrived(self.at(lx, p), self.ro + p)
                self.fwd_r(p).start()
                self.extra(lx, p)
                arrived(self.at(rx, 2 + p), self.ro + 6 + p)
                self.fwd_l(p).start()
                self.extra(rx, 2 + p)

            def second(p):
                arrived(self.at(lx, 2 + p), self.ro + 2 + p)
                self.extra(lx, 2 + p)
                arrived(self.at(rx, p), self.ro + 4 + p)
                self.extra(rx, p)

            def third(p):
                arrived(self.at(ox, p), self.ro + 8 + p)
                self.extra(ox, p)
                arrived(self.at(ox, 2 + p), self.ro + 10 + p)
                self.extra(ox, 2 + p)

            each(2, first)
            each(2, second)
            each(2, third)

        def drain(self):
            def one(p):
                self.own_r(p).wait_send()
                self.own_l(p).wait_send()

            each(4, one)

            def two(p):
                self.fwd_r(p).wait_send()
                self.fwd_l(p).wait_send()

            each(2, two)

    def first_tab(a, t):
        return tab_s[0, a, t]

    ub[...] = users[...].astype(BF16)

    def cast_slab(t):
        vb[t] = slab[t].astype(BF16)

    each(32, cast_slab)
    res[16] = jnp.zeros((128, 128), BF16)
    res_t[16] = jnp.zeros((128, 128), BF16)
    residuals(first_tab, lambda n: vals[0, n])

    ring = Ring(lambda c, j: c * 8 + j, 4, rb0)

    def chunk_grads(tab, c):
        each(2, lambda h: item_quad(tab, c * 2 + h))

    chunk_grads(first_tab, ox)
    ring.start_opp()
    chunk_grads(first_tab, rx)
    ring.start_mid_r()
    chunk_grads(first_tab, lx)
    ring.start_mid_l()
    chunk_grads(first_tab, x)

    move_s, move_r = take("s", 4), take("r", 4)
    move_tab = rc(tab_v, tab_in, move_s, move_r, swap)
    move_val = [rc(vals_out.at[i], vals_in.at[i], move_s + 1 + i, move_r + 1 + i, swap) for i in range(2)]
    move_users = rc(uf, uc, move_s + 3, move_r + 3, swap)

    @pl.when(moves)
    def _():
        move_tab.start()

        def one(n):
            vals_out[0, n] = vals[1, n].astype(F32)
            vals_out[1, n] = vals[2, n].astype(F32)

        each(16, one)
        move_val[0].start()

    @pl.when(keeps)
    def _():
        def one(n):
            vals_in[0, n] = vals[1, n].astype(F32)
            vals_in[1, n] = vals[2, n].astype(F32)

        each(16, one)
        tab_in[...] = tab_v[...]

    user_grads(first_tab)

    @pl.when(moves)
    def _():
        each(8, lambda a: uf.__setitem__(a, step_of(users[a], ug[a])))
        move_users.start()
        move_val[1].start()

    @pl.when(keeps)
    def _():
        each(8, lambda a: uc.__setitem__(a, step_of(users[a], ug[a])))

    ring.relay()

    part_s, part_r = take("s", 8), take("r", 8)
    shift_s, shift_r = take("s", 8), take("r", 4)

    def part_copy(j):
        return rc(vu0.at[j], part.at[j], part_s + j, part_r + j, across)

    def shift0(j):
        h, p = j // 4, j % 4
        target = ((base + strata - 2 * side + h) % strata, x * 2 + yhi)
        return rc(vu0.at[j], vn1.at[x * 8 + j], shift_s + j, shift_r + p, target)

    def shift_self(j):
        return pltpu.make_async_copy(vu0.at[j], vn1.at[x * 8 + j], rsem.at[shift_r + j % 4])

    def to_self(j):
        return (side == 0) & (j // 4 == 1)

    def summed(j, total):
        @pl.when(keeps)
        def _():
            vu0[j] = total
            part_copy(j).start()

        @pl.when(moves)
        def _():
            arrived(part.at[j], part_r + j)
            vu0[j] = step_of(slab[x * 8 + j], total + part[j])

            @pl.when(to_self(j))
            def _():
                shift_self(j).start()

            @pl.when(jnp.logical_not(to_self(j)))
            def _():
                shift0(j).start()

    ring.finish(summed)
    ring.drain()

    def gather(vn, arrive_r):
        sib_s, sib_r = take("s", 16), take("r", 16)

        def to_sib(chunk, p):
            spot = vn.at[chunk * 8 + core * 4 + p]
            return rc(spot, spot, sib_s + chunk * 4 + p, sib_r + chunk * 4 + p, sibling)

        def take_in(chunk, p):
            to_sib(chunk, p).start()
            t = chunk * 8 + core * 4 + p
            vb[t] = vn[t].astype(BF16)

        spread = Spread(vn, core, take_in)

        def own(p):
            arrived(vn.at[x * 8 + core * 4 + p], arrive_r + p)
            spread.own(p)
            take_in(x, p)

        each(4, own)
        spread.rest()

        def other(order):
            def one(p):
                t = order * 8 + (1 - core) * 4 + p
                arrived(vn.at[t], sib_r + order * 4 + p)
                vb[t] = vn[t].astype(BF16)

            each(4, one)

        for chunk in (x, lx, rx, ox):
            other(chunk)

        def drain():
            spread.drain()
            each(4, lambda c: each(4, lambda p: to_sib(c, p).wait_send()))

        return drain

    tab_copy = pltpu.make_async_copy(tab_in, tab_c, lsem.at[0])

    def row_step(k, vn, rb, sibs, done):
        def tab(a, t):
            return tab_c[k, a, t]

        for c in range(8):
            ub[c] = uc[c].astype(BF16)
        residuals(tab, lambda n: vals_in[k - 1, n])
        ring = Ring(lambda c, j: c * 8 + core * 4 + j, 2, rb)
        give_s, give_r = take("s", 16), take("r", 16)

        def give(c, p):
            return rc(
                grad.at[c * 8 + (1 - core) * 4 + p], sibs.at[c * 4 + p],
                give_s + c * 4 + p, give_r + c * 4 + p, sibling,
            )

        def compute(c):
            item_quad(tab, c * 2 + 1 - core)
            each(4, lambda p: give(c, p).start())
            item_quad(tab, c * 2 + core)

        def add(c):
            def one(p):
                arrived(sibs.at[c * 4 + p], give_r + c * 4 + p)
                t = c * 8 + core * 4 + p
                grad[t] = grad[t] + sibs[c * 4 + p]

            each(4, one)

        compute(ox)
        compute(rx)
        add(ox)
        ring.start_opp()
        compute(lx)
        add(rx)
        ring.start_mid_r()
        compute(x)
        add(lx)
        ring.start_mid_l()
        user_grads(tab)

        def update(a):
            uc[a] = step_of(uc[a], ug[a])

        each(8, update)
        if k == 2:
            back = rc(uc, uo, take("s", 1), take("r", 1), swap)

            @pl.when(moves)
            def _():
                back.start()

            @pl.when(keeps)
            def _():
                uo[...] = uc[...]

        ring.relay()
        add(x)

        def finish(p, total):
            done(p, step_of(vn[x * 8 + core * 4 + p], total))

        ring.finish(finish)
        ring.drain()
        each(4, lambda c: each(4, lambda p: give(c, p).wait_send()))
        if k == 2:
            return back

    drain1 = gather(vn1, shift_r)

    @pl.when(moves)
    def _():
        move_tab.wait_recv()
        move_val[0].wait_recv()
        move_users.wait_recv()
        move_tab.wait_send()
        move_val[0].wait_send()
        move_users.wait_send()

    tab_copy.start()
    tab_copy.wait()

    next_s, next_r = take("s", 4), take("r", 4)

    def shift1(p):
        target = ((s + strata - 2 * (1 - side)) % strata, x * 2 + yhi)
        return rc(vu1.at[p], vn2.at[x * 8 + core * 4 + p], next_s + p, next_r + p, target)

    def done1(p, value):
        vu1[p] = value
        shift1(p).start()

    row_step(1, vn1, rb1, sib1, done1)
    drain2 = gather(vn2, next_r)

    @pl.when(moves)
    def _():
        move_val[1].wait_recv()
        move_val[1].wait_send()

    last_s, last_r = take("s", 4), take("r", 4)
    cross_s, cross_r = take("s", 20), take("r", 20)

    def home(p):
        return rc(vu2.at[p], out.at[x * 8 + core * 4 + p], last_s + p, last_r + p, sibling)

    def cross_a(p):
        spot = out.at[x * 8 + core * 4 + p]
        return rc(spot, spot, cross_s + p, cross_r + p, across)

    def cross_b(c, p):
        spot = out.at[c * 8 + (1 - core) * 4 + p]
        k = 4 + c * 4 + p
        return rc(spot, spot, cross_s + k, cross_r + k, across)

    def emit(t):
        return pltpu.make_async_copy(out.at[t], items_out.at[t], lsem.at[1 + t])

    near = Spread(out, core, lambda c, p: emit(c * 8 + core * 4 + p).start())

    def far_extra(c, p):
        cross_b(c, p).start()
        emit(c * 8 + (1 - core) * 4 + p).start()

    far = Spread(out, 1 - core, far_extra)

    def done2(p, value):
        @pl.when(keeps)
        def _():
            out[x * 8 + core * 4 + p] = value
            near.own(p)
            cross_a(p).start()
            emit(x * 8 + core * 4 + p).start()

        @pl.when(moves)
        def _():
            vu2[p] = value
            home(p).start()

    back = row_step(2, vn2, rb2, sib2, done2)

    @pl.when(keeps)
    def _():
        def one(p):
            arrived(out.at[x * 8 + (1 - core) * 4 + p], last_r + p)
            far.own(p)
            far_extra(x, p)

        each(4, one)

    @pl.when(moves)
    def _():
        each(4, lambda p: home(p).wait_send())

        def one(p):
            t = x * 8 + core * 4 + p
            arrived(out.at[t], cross_r + p)
            near.own(p)
            emit(t).start()

        each(4, one)

    near.rest()

    @pl.when(keeps)
    def _():
        far.rest()

    @pl.when(moves)
    def _():
        def some(c):
            def one(p):
                t = c * 8 + (1 - core) * 4 + p
                arrived(out.at[t], cross_r + 4 + c * 4 + p)
                emit(t).start()

            each(4, one)

        for c in (x, lx, rx, ox):
            some(c)
        back.wait_recv()
        back.wait_send()

    users_copy = pltpu.make_async_copy(uo, users_out, lsem.at[0])
    users_copy.start()

    drain1()
    drain2()
    near.drain()
    each(4, lambda p: shift1(p).wait_send())

    @pl.when(keeps)
    def _():
        each(8, lambda j: part_copy(j).wait_send())
        far.drain()
        each(4, lambda p: cross_a(p).wait_send())
        each(4, lambda c: each(4, lambda p: cross_b(c, p).wait_send()))

    @pl.when(moves)
    def _():
        def one(j):
            @pl.when(jnp.logical_not(to_self(j)))
            def _():
                shift0(j).wait_send()

        each(8, one)

    each(32, lambda t: emit(t).wait())
    users_copy.wait()


def tables(coords, counts):
    order = jnp.arange(16, dtype=jnp.int32)
    live = order[None, :] < counts[:, None]
    a = jnp.clip(coords[:, 0], 0, 7)
    b = jnp.clip(coords[:, 1], 0, 31)
    hit = (
        (a[:, None, None, :] == jnp.arange(8, dtype=jnp.int32)[None, :, None, None])
        & (b[:, None, None, :] == jnp.arange(32, dtype=jnp.int32)[None, None, :, None])
        & live[:, None, None, :]
    )
    spot = jnp.min(jnp.where(hit, order, 16), axis=-1)
    wide = lambda v: jnp.broadcast_to(v[:, None, :], (3, 8, 16))
    return jnp.concatenate([spot, wide(a), wide(b), jnp.zeros((3, 8, 64), jnp.int32)], axis=-1)


def per_device(strata, user_factors, item_factors, tile_coords, tile_counts, tile_values):
    tab = tables(tile_coords[0, 0], tile_counts[0, 0])
    vmem = pl.BlockSpec(memory_space=pltpu.VMEM)
    smem = pl.BlockSpec(memory_space=pltpu.SMEM)
    anywhere = pl.BlockSpec(memory_space=pl.ANY)
    tiles = lambda n: pltpu.VMEM((n, 128, 256), F32)
    users, items = pl.pallas_call(
        lambda *refs: kernel(strata, *refs),
        out_shape=(
            jax.ShapeDtypeStruct((8, 128, 256), F32),
            jax.ShapeDtypeStruct((32, 128, 256), F32),
        ),
        in_specs=[smem, vmem, vmem, vmem, vmem],
        out_specs=(anywhere, anywhere),
        scratch_shapes=[
            tiles(8), tiles(8), tiles(8), tiles(8),
            pltpu.VMEM((8, 128, 256), BF16),
            pltpu.VMEM((32, 128, 256), BF16),
            pltpu.VMEM((17, 128, 128), BF16),
            pltpu.VMEM((17, 128, 128), BF16),
            pltpu.VMEM((512, 1024), BF16),
            tiles(32),
            pltpu.VMEM((2, 16, 128, 128), F32),
            pltpu.VMEM((2, 16, 128, 128), F32),
            pltpu.VMEM((3, 8, 128), jnp.int32),
            pltpu.SMEM((3, 8, 128), jnp.int32),
            tiles(24), tiles(12), tiles(12), tiles(16), tiles(16),
            tiles(8), tiles(8), tiles(4), tiles(4),
            tiles(32), tiles(32), tiles(32),
            pltpu.SemaphoreType.DMA((SEMS,)),
            pltpu.SemaphoreType.DMA((SEMS,)),
            pltpu.SemaphoreType.DMA((33,)),
        ],
        compiler_params=pltpu.CompilerParams(
            collective_id=0, has_side_effects=True, vmem_limit_bytes=67043328
        ),
    )(
        tab, tab,
        user_factors.reshape(8, 128, 256),
        item_factors.reshape(32, 128, 256),
        tile_values[0, 0],
    )
    return users.reshape(1024, 256), items.reshape(4096, 256)


def solution(mesh):
    strata = mesh.shape["strat"]
    placed = (
        P(("strat", "grp"), None),
        P("strat", None),
        P("strat", "grp", None, None, None),
        P("strat", "grp", None),
        P("strat", "grp", None, None, None, None),
    )
    return jax.shard_map(
        lambda *args: per_device(strata, *args),
        mesh=mesh,
        in_specs=placed,
        out_specs=(P(("strat", "grp"), None), P("strat", None)),
        check_vma=False,
    )
```

```python
import jax
import jax.numpy as jnp
from jax import lax
from jax.experimental import pallas as pl
from jax.experimental.pallas import tpu as pltpu
from jax.sharding import PartitionSpec as P

MESH = pl.DeviceIdType.MESH
F32 = jnp.float32
BF16 = jnp.bfloat16
RATE = 0.003
DECAY = 0.05
SEMS = 256
VMEM_BYTES = 54 * 2**20


def step_of(value, grad):
    return value - RATE * (DECAY * value - grad)


def kernel(
    strata, coords, counts, users_in, slab_in, vals_in_hbm, uo, out,
    users, slab, vals, tab_v, uf, uc, ug, ub, vb, res, res_t, lhs, grad, vals_out, vals_in, tab_in, tab_c,
    rb0, rb1, rb2, sib1, sib2, part, vu0, vu1, vu2, rel, vn1, vn2, ssem, rsem, lsem,
):
    s, g = lax.axis_index("strat"), lax.axis_index("grp")
    core, yhi, x, ylo = s % 2, (s // 2) % 2, g // 2, g % 2
    base = s - core
    side = (ylo + yhi) % 2
    keeps = core == side
    moves = core != side
    rx, lx, ox = (x + 1) % 4, (x + 3) % 4, (x + 2) % 4
    right, left = (s, rx * 2 + ylo), (s, lx * 2 + ylo)
    sibling = (base + 1 - core, g)
    across = (s, x * 2 + 1 - ylo)
    swap = (base + 1 - core, x * 2 + 1 - ylo)
    ahead = (s + strata - 2) % strata
    behind = (s + 2) % strata

    def fetch(src, dst, k):
        copy = pltpu.make_async_copy(src, dst, lsem.at[k])
        copy.start()
        return copy

    get_vals = [fetch(vals_in_hbm.at[k], vals.at[k], k) for k in (1, 0, 2)]
    get_users = fetch(users_in, users, 3)
    get_slab = fetch(slab_in, slab, 4)

    barrier = pltpu.get_barrier_semaphore()

    def greet(device):
        pl.semaphore_signal(barrier, inc=1, device_id=device, device_id_type=MESH)

    for device in (right, left, sibling, across, swap):
        greet(device)

    @pl.when(side == 1)
    def _():
        greet((ahead, x * 2 + 1 - ylo))
        greet((behind, x * 2 + 1 - ylo))
        greet(((s + strata - 1 + 2 * core) % strata, x * 2 + 1 - ylo))

    rows = lax.broadcasted_iota(jnp.int32, (8, 128), 0)
    cols = lax.broadcasted_iota(jnp.int32, (8, 128), 1)

    def user_tile(k, n):
        return jnp.clip(coords[k, 0, n], 0, 7)

    def item_tile(k, n):
        return jnp.clip(coords[k, 1, n], 0, 31)

    for k in range(3):
        table = jnp.full((8, 128), 16, jnp.int32)
        for n in range(16):
            a, b = user_tile(k, n), item_tile(k, n)
            spot = jnp.where(n < counts[k], b, 1000)
            table = jnp.where((rows == a) & (cols == spot), n, table)
            table = jnp.where(cols == 32 + n, a, table)
            table = jnp.where(cols == 48 + n, b, table)
        tab_v[k] = table
    tab_copy0 = fetch(tab_v.at[0], tab_c.at[0], 5)

    pl.semaphore_wait(barrier, 5 + 3 * side)

    def rc(src, dst, si, ri, device):
        return pltpu.make_async_remote_copy(
            src_ref=src, dst_ref=dst, send_sem=ssem.at[si], recv_sem=rsem.at[ri],
            device_id=device, device_id_type=MESH,
        )

    def arrived(ref, ri):
        rc(ref, ref, 0, ri, right).wait_recv()

    taken = {"s": 0, "r": 0}

    def take(kind, n):
        taken[kind] += n
        assert taken[kind] <= SEMS
        return taken[kind] - n

    def each(n, body):
        @pl.loop(0, n)
        def _(i):
            body(i)

    def residuals(user_at, item_at, values):
        def one(n):
            u = ub[user_at(n)]
            v = vb[item_at(n)]
            guess = lax.dot_general(u, v, (((1,), (1,)), ((), ())), preferred_element_type=F32)
            left_over = values(n).astype(F32) - guess
            res[n] = left_over.astype(BF16)
            res_t[n] = left_over.T.astype(BF16)

        each(4, lambda i: [one(i * 4 + j) for j in range(4)])

    def item_quad(tab, q):
        for i in range(4):
            for a in range(8):
                lhs[i * 128:(i + 1) * 128, a * 128:(a + 1) * 128] = res_t[tab(a, q * 4 + i)]
        total = jnp.dot(lhs[...], ub[...].reshape(1024, 256), preferred_element_type=F32)
        grad[pl.ds(q * 4, 4)] = total.reshape(4, 128, 256)

    def user_grads(tab):
        def one(w):
            half, c = w // 4, w % 4
            for i in range(4):
                for j in range(8):
                    lhs[i * 128:(i + 1) * 128, j * 128:(j + 1) * 128] = res[tab(half * 4 + i, c * 8 + j)]
            block = vb[pl.ds(c * 8, 8)].reshape(1024, 256)
            total = jnp.dot(lhs[...], block, preferred_element_type=F32)
            spot = pl.ds(half * 4, 4)
            ug[spot] = ug[spot] + total.reshape(4, 128, 256)

        ug[...] = jnp.zeros_like(ug)
        each(8, one)

    class Ring:
        def __init__(self, tile, m, rb):
            self.tile, self.m, self.rb = tile, m, rb
            self.so, self.ro = take("s", 6 * m), take("r", 6 * m)

        def go(self, chunk, j, slot, k, device):
            return rc(grad.at[self.tile(chunk, j)], self.rb.at[slot], self.so + k, self.ro + slot, device)

        def opp_r(self, j):
            return self.go(ox, j, j, j, right)

        def opp_l(self, j):
            return self.go(ox, self.m + j, self.m + j, self.m + j, left)

        def mid_r(self, j):
            return self.go(rx, self.m + j, 3 * self.m + j, 2 * self.m + j, right)

        def mid_l(self, j):
            return self.go(lx, j, 4 * self.m + j, 3 * self.m + j, left)

        def end_r(self, j):
            return self.go(rx, j, 2 * self.m + j, 4 * self.m + j, right)

        def end_l(self, j):
            return self.go(lx, self.m + j, 5 * self.m + j, 5 * self.m + j, left)

        def landed(self, slot):
            arrived(self.rb.at[slot], self.ro + slot)

        def start_opp(self):
            each(self.m, lambda j: (self.opp_r(j).start(), self.opp_l(j).start()))

        def start_mid_r(self):
            each(self.m, lambda j: self.mid_r(j).start())

        def start_mid_l(self):
            each(self.m, lambda j: self.mid_l(j).start())

        def relay(self):
            def one(j):
                self.landed(j)
                spot = self.tile(rx, j)
                grad[spot] = grad[spot] + self.rb[j]
                self.end_r(j).start()
                self.landed(self.m + j)
                spot = self.tile(lx, self.m + j)
                grad[spot] = grad[spot] + self.rb[self.m + j]
                self.end_l(j).start()

            each(self.m, one)

        def finish(self, done):
            m = self.m

            def one(j):
                self.landed(4 * m + j)
                self.landed(2 * m + j)
                done(j, grad[self.tile(x, j)] + self.rb[2 * m + j] + self.rb[4 * m + j])
                self.landed(3 * m + j)
                self.landed(5 * m + j)
                done(m + j, grad[self.tile(x, m + j)] + self.rb[3 * m + j] + self.rb[5 * m + j])

            each(m, one)

        def drain(self):
            def one(j):
                for f in (self.opp_r, self.opp_l, self.mid_r, self.mid_l, self.end_r, self.end_l):
                    f(j).wait_send()

            each(self.m, one)

    class Spread:
        def __init__(self, buf, half, extra):
            self.buf, self.half, self.extra = buf, half, extra
            self.so, self.ro = take("s", 12), take("r", 12)

        def at(self, chunk, p):
            return self.buf.at[chunk * 8 + self.half * 4 + p]

        def own_r(self, p):
            return rc(self.at(x, p), self.at(x, p), self.so + p, self.ro + p, right)

        def own_l(self, p):
            return rc(self.at(x, p), self.at(x, p), self.so + 4 + p, self.ro + 4 + p, left)

        def fwd_r(self, p):
            return rc(self.at(lx, p), self.at(lx, p), self.so + 8 + p, self.ro + 8 + p, right)

        def fwd_l(self, p):
            return rc(self.at(rx, 2 + p), self.at(rx, 2 + p), self.so + 10 + p, self.ro + 10 + p, left)

        def own(self, p):
            self.own_r(p).start()
            self.own_l(p).start()

        def rest(self):
            def first(p):
                arrived(self.at(lx, p), self.ro + p)
                self.fwd_r(p).start()
                self.extra(lx, p)
                arrived(self.at(rx, 2 + p), self.ro + 6 + p)
                self.fwd_l(p).start()
                self.extra(rx, 2 + p)

            def second(p):
                arrived(self.at(lx, 2 + p), self.ro + 2 + p)
                self.extra(lx, 2 + p)
                arrived(self.at(rx, p), self.ro + 4 + p)
                self.extra(rx, p)

            def third(p):
                arrived(self.at(ox, p), self.ro + 8 + p)
                self.extra(ox, p)
                arrived(self.at(ox, 2 + p), self.ro + 10 + p)
                self.extra(ox, 2 + p)

            each(2, first)
            each(2, second)
            each(2, third)

        def drain(self):
            def one(p):
                self.own_r(p).wait_send()
                self.own_l(p).wait_send()

            each(4, one)

            def two(p):
                self.fwd_r(p).wait_send()
                self.fwd_l(p).wait_send()

            each(2, two)

    def first_tab(a, t):
        return tab_c[0, a, t]

    move_s, move_r = take("s", 4), take("r", 4)
    move_tab = rc(tab_v, tab_in, move_s, move_r, swap)
    move_val = [rc(vals_out.at[i], vals_in.at[i], move_s + 1 + i, move_r + 1 + i, swap) for i in range(2)]
    move_users = rc(uf, uc, move_s + 3, move_r + 3, swap)

    def widen(dst, k):
        each(4, lambda i: dst.__setitem__((k - 1, pl.ds(i * 4, 4)), vals[k, pl.ds(i * 4, 4)].astype(F32)))

    get_vals[0].wait()

    @pl.when(moves)
    def _():
        widen(vals_out, 1)
        move_val[0].start()
        move_tab.start()

    get_users.wait()
    ub[...] = users[...].astype(BF16)
    get_slab.wait()

    def cast_slab(t):
        vb[t] = slab[t].astype(BF16)

    each(32, cast_slab)
    get_vals[1].wait()
    residuals(lambda n: user_tile(0, n), lambda n: item_tile(0, n), lambda n: vals[0, n])
    res[16] = jnp.zeros((128, 128), BF16)
    res_t[16] = jnp.zeros((128, 128), BF16)
    tab_copy0.wait()

    ring = Ring(lambda c, j: c * 8 + j, 4, rb0)

    def chunk_grads(tab, c):
        each(2, lambda h: item_quad(tab, c * 2 + h))

    chunk_grads(first_tab, ox)
    ring.start_opp()
    chunk_grads(first_tab, rx)
    ring.start_mid_r()
    chunk_grads(first_tab, lx)
    ring.start_mid_l()
    chunk_grads(first_tab, x)

    user_grads(first_tab)

    @pl.when(moves)
    def _():
        each(8, lambda a: uf.__setitem__(a, step_of(users[a], ug[a])))
        move_users.start()

    @pl.when(keeps)
    def _():
        each(8, lambda a: uc.__setitem__(a, step_of(users[a], ug[a])))
        widen(vals_in, 1)

    get_vals[2].wait()
    ring.relay()

    part_s, part_r = take("s", 8), take("r", 8)
    shift_s, shift_r = take("s", 8), take("r", 4)

    def part_copy(j):
        return rc(vu0.at[j], part.at[j], part_s + j, part_r + j, across)

    def shift0(j):
        h, p = j // 4, j % 4
        target = ((base + strata - 2 * side + h) % strata, x * 2 + yhi)
        return rc(vu0.at[j], vn1.at[x * 8 + j], shift_s + j, shift_r + p, target)

    def shift_self(j):
        return pltpu.make_async_copy(vu0.at[j], vn1.at[x * 8 + j], rsem.at[shift_r + j % 4])

    def to_self(j):
        return (side == 0) & (j // 4 == 1)

    def summed(j, total):
        @pl.when(keeps)
        def _():
            vu0[j] = total
            part_copy(j).start()

        @pl.when(moves)
        def _():
            arrived(part.at[j], part_r + j)
            vu0[j] = step_of(slab[x * 8 + j], total + part[j])

            @pl.when(to_self(j))
            def _():
                shift_self(j).start()

            @pl.when(jnp.logical_not(to_self(j)))
            def _():
                shift0(j).start()

    ring.finish(summed)

    @pl.when(moves)
    def _():
        widen(vals_out, 2)
        move_val[1].start()
        move_tab.wait_recv()
        fetch(tab_in.at[pl.ds(1, 2)], tab_c.at[pl.ds(1, 2)], 0)
        move_users.wait_recv()

    @pl.when(keeps)
    def _():
        fetch(tab_v.at[pl.ds(1, 2)], tab_c.at[pl.ds(1, 2)], 0)
        widen(vals_in, 2)

    def cast_users():
        each(8, lambda a: ub.__setitem__(a, uc[a].astype(BF16)))

    cast_users()
    ring.drain()
    pltpu.make_async_copy(tab_v.at[pl.ds(1, 2)], tab_c.at[pl.ds(1, 2)], lsem.at[0]).wait()

    def gather(vn, arrive_r):
        sib_s, sib_r = take("s", 16), take("r", 16)

        def to_sib(chunk, p):
            spot = vn.at[chunk * 8 + core * 4 + p]
            return rc(spot, spot, sib_s + chunk * 4 + p, sib_r + chunk * 4 + p, sibling)

        def take_in(chunk, p):
            to_sib(chunk, p).start()
            t = chunk * 8 + core * 4 + p
            vb[t] = vn[t].astype(BF16)

        spread = Spread(vn, core, take_in)

        def own(p):
            arrived(vn.at[x * 8 + core * 4 + p], arrive_r + p)
            spread.own(p)
            take_in(x, p)

        each(4, own)
        spread.rest()

        def other(order):
            def one(p):
                t = order * 8 + (1 - core) * 4 + p
                arrived(vn.at[t], sib_r + order * 4 + p)
                vb[t] = vn[t].astype(BF16)

            each(4, one)

        for chunk in (x, lx, rx, ox):
            other(chunk)

        def drain():
            spread.drain()
            each(4, lambda c: each(4, lambda p: to_sib(c, p).wait_send()))

        return drain

    def row_step(k, vn, rb, sibs, done):
        def tab(a, t):
            return tab_c[k, a, t]

        residuals(lambda n: tab(0, 32 + n), lambda n: tab(0, 48 + n), lambda n: vals_in[k - 1, n])
        ring = Ring(lambda c, j: c * 8 + core * 4 + j, 2, rb)
        give_s, give_r = take("s", 16), take("r", 16)

        def give(c, p):
            return rc(
                grad.at[c * 8 + (1 - core) * 4 + p], sibs.at[c * 4 + p],
                give_s + c * 4 + p, give_r + c * 4 + p, sibling,
            )

        def theirs(c):
            item_quad(tab, c * 2 + 1 - core)
            each(4, lambda p: give(c, p).start())

        def ours(c):
            item_quad(tab, c * 2 + core)

        def add(c):
            def one(p):
                arrived(sibs.at[c * 4 + p], give_r + c * 4 + p)
                t = c * 8 + core * 4 + p
                grad[t] = grad[t] + sibs[c * 4 + p]

            each(4, one)

        theirs(ox)
        ours(ox)
        theirs(rx)
        add(ox)
        ring.start_opp()
        ours(rx)
        theirs(lx)
        add(rx)
        ring.start_mid_r()
        ours(lx)
        theirs(x)
        add(lx)
        ring.start_mid_l()
        ours(x)
        user_grads(tab)

        def update(a):
            uc[a] = step_of(uc[a], ug[a])

        each(8, update)
        if k == 1:
            cast_users()
        if k == 2:
            back = rc(uc, uo, take("s", 1), take("r", 1), swap)

            @pl.when(moves)
            def _():
                back.start()

            @pl.when(keeps)
            def _():
                uo[...] = uc[...]

        ring.relay()
        add(x)

        def finish(p, total):
            done(p, step_of(vn[x * 8 + core * 4 + p], total))

        ring.finish(finish)
        ring.drain()
        each(4, lambda c: each(4, lambda p: give(c, p).wait_send()))
        if k == 2:
            return back

    drain1 = gather(vn1, shift_r)

    @pl.when(moves)
    def _():
        move_val[0].wait_recv()
        move_tab.wait_send()
        move_val[0].wait_send()
        move_users.wait_send()

    next_s, next_r = take("s", 4), take("r", 4)

    rel_s, rel_r = take("s", 4), take("r", 4)

    def shift1(p):
        return rc(vu1.at[p], vn2.at[x * 8 + core * 4 + p], next_s + p, next_r + p, across)

    def shift2(p):
        return rc(vu1.at[p], rel.at[p], next_s + p, rel_r + p, across)

    def shift3(p):
        target = (ahead, x * 2 + 1 - ylo)
        return rc(rel.at[p], vn2.at[x * 8 + core * 4 + p], rel_s + p, next_r + p, target)

    def done1(p, value):
        vu1[p] = value

        @pl.when(side == 1)
        def _():
            shift1(p).start()

        @pl.when(side == 0)
        def _():
            shift2(p).start()

    row_step(1, vn1, rb1, sib1, done1)

    @pl.when(side == 1)
    def _():
        for p in (0, 2, 1, 3):
            arrived(rel.at[p], rel_r + p)
            shift3(p).start()
    drain2 = gather(vn2, next_r)

    @pl.when(moves)
    def _():
        move_val[1].wait_recv()
        move_val[1].wait_send()

    last_s, last_r = take("s", 4), take("r", 4)
    cross_s, cross_r = take("s", 20), take("r", 20)

    def home(p):
        return rc(vu2.at[p], out.at[x * 8 + core * 4 + p], last_s + p, last_r + p, sibling)

    def cross_a(p):
        spot = out.at[x * 8 + core * 4 + p]
        return rc(spot, spot, cross_s + p, cross_r + p, across)

    def cross_b(c, p):
        spot = out.at[c * 8 + (1 - core) * 4 + p]
        k = 4 + c * 4 + p
        return rc(spot, spot, cross_s + k, cross_r + k, across)

    near = Spread(out, core, lambda c, p: None)

    def far_extra(c, p):
        cross_b(c, p).start()

    far = Spread(out, 1 - core, far_extra)

    def done2(p, value):
        @pl.when(keeps)
        def _():
            out[x * 8 + core * 4 + p] = value
            near.own(p)
            cross_a(p).start()

        @pl.when(moves)
        def _():
            vu2[p] = value
            home(p).start()

    back = row_step(2, vn2, rb2, sib2, done2)

    @pl.when(keeps)
    def _():
        def one(p):
            arrived(out.at[x * 8 + (1 - core) * 4 + p], last_r + p)
            far.own(p)
            far_extra(x, p)

        each(4, one)

    @pl.when(moves)
    def _():
        each(4, lambda p: home(p).wait_send())

        def one(p):
            t = x * 8 + core * 4 + p
            arrived(out.at[t], cross_r + p)
            near.own(p)

        each(4, one)

    near.rest()

    @pl.when(keeps)
    def _():
        far.rest()

    @pl.when(moves)
    def _():
        def some(c):
            def one(p):
                t = c * 8 + (1 - core) * 4 + p
                arrived(out.at[t], cross_r + 4 + c * 4 + p)

            each(4, one)

        for c in (x, lx, rx, ox):
            some(c)
        back.wait_recv()
        back.wait_send()

    drain1()
    drain2()
    near.drain()
    each(4, lambda p: shift2(p).wait_send())

    @pl.when(side == 1)
    def _():
        each(4, lambda p: shift3(p).wait_send())

    @pl.when(keeps)
    def _():
        each(8, lambda j: part_copy(j).wait_send())
        far.drain()
        each(4, lambda p: cross_a(p).wait_send())
        each(4, lambda c: each(4, lambda p: cross_b(c, p).wait_send()))

    @pl.when(moves)
    def _():
        def one(j):
            @pl.when(jnp.logical_not(to_self(j)))
            def _():
                shift0(j).wait_send()

        each(8, one)


def per_device(strata, user_factors, item_factors, tile_coords, tile_counts, tile_values):
    vmem = pl.BlockSpec(memory_space=pltpu.VMEM)
    smem = pl.BlockSpec(memory_space=pltpu.SMEM)
    anywhere = pl.BlockSpec(memory_space=pl.ANY)
    tiles = lambda n: pltpu.VMEM((n, 128, 256), F32)
    users, items = pl.pallas_call(
        lambda *refs: kernel(strata, *refs),
        out_shape=(
            pltpu.VMEM((8, 128, 256), F32),
            pltpu.VMEM((32, 128, 256), F32),
        ),
        in_specs=[smem, smem, anywhere, anywhere, anywhere],
        out_specs=(vmem, vmem),
        scratch_shapes=[
            tiles(8), tiles(32), pltpu.VMEM((3, 16, 128, 128), BF16), pltpu.VMEM((3, 8, 128), jnp.int32),
            tiles(8), tiles(8), tiles(8),
            pltpu.VMEM((8, 128, 256), BF16),
            pltpu.VMEM((32, 128, 256), BF16),
            pltpu.VMEM((17, 128, 128), BF16),
            pltpu.VMEM((17, 128, 128), BF16),
            pltpu.VMEM((512, 1024), BF16),
            tiles(32),
            pltpu.VMEM((2, 16, 128, 128), F32),
            pltpu.VMEM((2, 16, 128, 128), F32),
            pltpu.VMEM((3, 8, 128), jnp.int32),
            pltpu.SMEM((3, 8, 128), jnp.int32),
            tiles(24), tiles(12), tiles(12), tiles(16), tiles(16),
            tiles(8), tiles(8), tiles(4), tiles(4), tiles(4),
            tiles(32), tiles(32),
            pltpu.SemaphoreType.DMA((SEMS,)),
            pltpu.SemaphoreType.DMA((SEMS,)),
            pltpu.SemaphoreType.DMA((6,)),
        ],
        compiler_params=pltpu.CompilerParams(
            collective_id=0, has_side_effects=True, vmem_limit_bytes=VMEM_BYTES
        ),
    )(
        tile_coords[0, 0], tile_counts[0, 0],
        user_factors.reshape(8, 128, 256),
        item_factors.reshape(32, 128, 256),
        tile_values[0, 0],
    )
    return users.reshape(1024, 256), items.reshape(4096, 256)


def solution(mesh):
    strata = mesh.shape["strat"]
    placed = (
        P(("strat", "grp"), None),
        P("strat", None),
        P("strat", "grp", None, None, None),
        P("strat", "grp", None),
        P("strat", "grp", None, None, None, None),
    )
    return jax.shard_map(
        lambda *args: per_device(strata, *args),
        mesh=mesh,
        in_specs=placed,
        out_specs=(P(("strat", "grp"), None), P("strat", None)),
        check_vma=False,
    )
```
